256 devices in a mesh: gx: 16 (over z, core), gy: 8 (over y_lo, x), col: 2 (over y_hi).
Axes of the slice: x: 4, y: 4 (y_hi: 2, y_lo: 2; y = y_hi * 2 + y_lo), z: 8, core: 2. Of those that a mesh axis runs over, the one named last changes fastest.
Arguments:
- field: bfloat16 [64, 32, 128, 128], P(None, 'gx', 'gy'), may hold values from -6 to 6
- first_weight: bfloat16 [64, 64, 3, 3, 3], P('col'), may hold values from -0.21875 to 0.21875
- second_weight: bfloat16 [64, 64, 3, 3, 3], P('col'), may hold values from -0.21875 to 0.21875
- up_weight: bfloat16 [32, 64, 4, 4, 4], P('col'), may hold values from -0.375 to 0.375
Outputs:
- upsampled: bfloat16 [32, 64, 256, 256], P('col', 'gx', 'gy')
The draws below stay inside these ranges and needn't reach their ends.
All inputs are finite; a program needn't handle non-finite values.
Results may differ from the reference program's by a relative error of at most 0.0059.
Values may be sent and summed in bfloat16 or wider, within the bound.
A program may use at most 64 MiB of HBM per device.

```python
import jax
import jax.numpy as jnp
from jax import lax

C = 64
COUT = 32
NX = 32
NY = 128
NZ = 128


def steps_of(key, shape, shards, smallest, top_value):
    gain = 1.0
    for position, parts in shards:
        steps = jax.random.uniform(jax.random.fold_in(jax.random.fold_in(key, 6), position), (parts,), jnp.float32, smallest / len(shards), top_value / len(shards))
        gain = gain * jnp.repeat(jnp.exp(steps), shape[position] // parts).reshape((-1,) + (1,) * (len(shape) - 1 - position))
    return gain


def noise(own_key, dims, deviation, most, split=(), held_as=jnp.bfloat16):
    loudness = steps_of(own_key, dims, split, -0.22, 0.18) if split else 1.0
    array = jax.random.normal(own_key, dims, jnp.float32) * deviation * loudness
    return jnp.minimum(jnp.maximum(array, -most), most).astype(held_as)


def setup_inputs(seed: int = 0) -> dict:
    streams_of = jax.random.split(jax.random.key(seed), 5)
    field = noise(streams_of[0], (C, NX, NY, NZ), 1.0, 6.0, ((1, 16), (2, 8)))
    first_weight = noise(streams_of[1], (C, C, 3, 3, 3), (27 * C // 2) ** -0.5, 0.21875, ((0, 2),))
    second_weight = noise(streams_of[2], (C, C, 3, 3, 3), (27 * C // 2) ** -0.5, 0.21875, ((0, 2),))
    up_weight = noise(streams_of[3], (COUT, C, 4, 4, 4), (4 * C) ** -0.5, 0.375, ((0, 2),))
    return dict(field=field, first_weight=first_weight, second_weight=second_weight, up_weight=up_weight)


def convolve(padded, kernel):
    return lax.conv_general_dilated(padded[None], kernel, (1, 1, 1), "VALID", dimension_numbers=("NCDHW", "OIDHW", "NCDHW"), preferred_element_type=jnp.float32)[0]


def upsample(padded, weight):
    cells_x = padded.shape[1] - 2
    cells_y = padded.shape[2] - 2
    cells_z = padded.shape[3] - 2
    channels_out = weight.shape[0]
    results = []
    for parity in range(8):
        along_x = parity // 4
        along_y = parity // 2 % 2
        along_z = parity % 2
        piece = padded[:, along_x:along_x + cells_x + 1, along_y:along_y + cells_y + 1, along_z:along_z + cells_z + 1]
        kernel = weight[:, :, 3 - along_x::-2, 3 - along_y::-2, 3 - along_z::-2]
        results.append(convolve(piece, kernel).astype(jnp.bfloat16))
    stacked = jnp.stack(results).reshape(2, 2, 2, channels_out, cells_x, cells_y, cells_z)
    return stacked.transpose(3, 4, 0, 5, 1, 6, 2).reshape(channels_out, 2 * cells_x, 2 * cells_y, 2 * cells_z)


def wrapped(field):
    return jnp.pad(field, ((0, 0), (1, 1), (1, 1), (1, 1)), mode="wrap")


def reference(field, first_weight, second_weight, up_weight):
    first = jnp.maximum(convolve(wrapped(field), first_weight), 0.0).astype(jnp.bfloat16)
    second = jnp.maximum(convolve(wrapped(first), second_weight), 0.0).astype(jnp.bfloat16)
    return upsample(wrapped(second), up_weight)
```

```python
import functools

import jax
import jax.numpy as jnp
from jax import lax
from jax.experimental import pallas as pl
from jax.experimental.pallas import tpu as pltpu
from jax.sharding import PartitionSpec as P

C = 64
NZ = 128
ROWS = 16
DEPTH = 3
MESH = pl.DeviceIdType.MESH
MIDDLE = tuple(range(1, 15))
BORDER = (-2, -1, 0, 15, 16, 17)
MIDDLE_2 = tuple(range(2, 14))
BORDER_2 = (-1, 0, 1, 14, 15, 16)
MIDDLE_3 = tuple(range(3, 13))
BORDER_3 = (0, 1, 2, 13, 14, 15)
COPIES = 28


def pairs(items):
    return [items[i : i + 2] for i in range(0, len(items), 2)]


def block(first, count):
    return pl.ds(first * C, count * C)


def taps_matmul(weight, cells, source, span):
    columns = [
        jnp.concatenate([source[layer, block(row, span), :] for layer in layers], axis=0) for layers, row in cells
    ]
    return jnp.dot(weight, jnp.concatenate(columns, axis=1), preferred_element_type=jnp.float32)


def convolve(weight_ref, source, source_at, target, target_at, layer, rows):
    weight = weight_ref[...]
    for pair in pairs(rows):
        cells = [([layer + k + source_at for k in (-1, 0, 1)], row - 1 + source_at) for row in pair]
        taps = taps_matmul(weight, cells, source, 3)
        for i, row in enumerate(pair):
            for half in range(2):
                tap = taps[half * 96 : half * 96 + 96, i * NZ : (i + 1) * NZ]
                value = pltpu.roll(tap[:32], 1, 1) + tap[32:64] + pltpu.roll(tap[64:], NZ - 1, 1)
                start = (row + target_at) * C + half * 32
                target[layer + target_at, start : start + 32, :] = jnp.maximum(value, 0.0).astype(jnp.bfloat16)


def refine(core, weight_ref, source, fine, layer, rows):
    for along_x in range(2):
        flat = 2 * layer + along_x
        plane = flat + core * (3 - 2 * flat)
        for along_y in range(2):
            weight = weight_ref[2 * along_x + along_y]
            for pair in pairs(rows):
                cells = [([layer + along_x, layer + along_x + 1], row + along_y) for row in pair]
                taps = taps_matmul(weight, cells, source, 2)
                for i, row in enumerate(pair):
                    tap = taps[:, i * NZ : (i + 1) * NZ]
                    even = pltpu.roll(tap[48:], 1, 1) + tap[16:32]
                    odd = tap[32:48] + pltpu.roll(tap[:16], NZ - 1, 1)
                    line = pl.ds(2 * row + along_y, 16, stride=32)
                    fine[plane, 0, line, :] = even
                    fine[plane, 1, line, :] = odd


def kernel(
    field_ref, w1_ref, w2_ref, up_ref, out_ref,
    spread, cells, first, second, fine, w1, w2, send, recv,
):
    gx = lax.axis_index("gx")
    gy = lax.axis_index("gy")
    col = lax.axis_index("col")
    core = lax.rem(gx, 2)
    sign = 1 - 2 * core
    partner = {"gx": gx + sign}
    outer = {"gx": lax.rem(gx + 16 - sign, 16)}
    far = {"gx": lax.rem(gx + 16 + 2 * sign, 16)}
    far_back = {"gx": lax.rem(gx + 16 - 2 * sign, 16)}
    up = {"gy": lax.rem(gy + 1, 8)}
    down = {"gy": lax.rem(gy + 7, 8)}
    other = {"col": 1 - col}

    barrier = pltpu.get_barrier_semaphore()
    for device in (partner, outer, far, far_back, up, down, other):
        pl.semaphore_signal(barrier, inc=1, device_id=device, device_id_type=MESH)

    def copy(number, source, target, device):
        return pltpu.make_async_remote_copy(
            src_ref=source,
            dst_ref=target,
            send_sem=send.at[number],
            recv_sem=recv.at[number],
            device_id=device,
            device_id_type=MESH,
        )

    def rows_of(buffer, at, source_layer, source_row, target_layer, target_row, count):
        return (
            buffer.at[source_layer + at, block(source_row + at, count)],
            buffer.at[target_layer + at, block(target_row + at, count)],
        )

    mine = pl.ds(pl.multiple_of(col * 96, 96), 96)

    def same(ref):
        return ref.at[mine], ref.at[mine]

    a = functools.partial(rows_of, cells, 3)
    f = functools.partial(rows_of, first, 2)
    s = functools.partial(rows_of, second, 1)
    both = pl.ds(3, 2)
    copies = [
        copy(0, *same(w1), other),
        copy(1, *same(w2), other),
        copy(2, *a(1, 0, 2, 0, 16), partner),
        copy(3, *a(0, 0, -1, 0, 3), outer),
        copy(4, *a(0, 13, -1, 13, 3), outer),
        copy(5, *a(1, 0, -2, 0, 3), outer),
        copy(6, *a(1, 13, -2, 13, 3), outer),
        copy(7, *a(1, 0, -3, 0, 3), far),
        copy(8, *a(1, 13, -3, 13, 3), far),
        copy(9, *a(0, 3, -1, 3, 10), outer),
        copy(10, *a(1, 3, -2, 3, 10), outer),
        copy(11, *a(1, 3, -3, 3, 10), far),
        copy(12, cells.at[both, block(3, 3)], cells.at[both, block(19, 3)], down),
        copy(13, cells.at[both, block(16, 3)], cells.at[both, block(0, 3)], up),
        copy(14, *a(-1, 0, -1, 16, 3), down),
        copy(15, *a(-1, 13, -1, -3, 3), up),
        copy(16, *a(-2, 0, -2, 16, 3), down),
        copy(17, *a(-2, 13, -2, -3, 3), up),
        copy(18, *a(-3, 0, -3, 16, 3), down),
        copy(19, *a(-3, 13, -3, -3, 3), up),
        copy(20, *a(1, -3, 2, -3, 3), partner),
        copy(21, *a(1, 16, 2, 16, 3), partner),
        copy(22, *f(1, 1, 2, 1, 14), partner),
        copy(23, *f(1, -2, 2, -2, 3), partner),
        copy(24, *f(1, 15, 2, 15, 3), partner),
        copy(25, *s(1, 2, 2, 2, 12), partner),
        copy(26, *s(1, -1, 2, -1, 3), partner),
        copy(27, *s(1, 14, 2, 14, 3), partner),
    ]

    def start(*numbers):
        for number in numbers:
            copies[number].start()

    def arrive(*numbers):
        for number in numbers:
            copies[number].wait_recv()

    def assemble(source, target):
        for along_x in range(3):
            for along_y in range(3):
                piece = source[along_x + core * (2 - 2 * along_x), along_y].reshape(96, C)
                k = 3 * along_x + along_y
                target[mine, k * C : (k + 1) * C] = piece

    def lay_out(rows):
        for layer in range(2):
            plane = layer + core * (1 - 2 * layer)
            for row in rows:
                value = spread[pl.ds(plane * ROWS + row, C, stride=2 * ROWS), :]
                cells[layer + 3, block(row + 3, 1), :] = value.astype(jnp.bfloat16)

    assemble(w1_ref, w1)
    for i in range(8):
        spread[i * 256 : (i + 1) * 256, :] = field_ref[8 * i : 8 * i + 8].astype(jnp.float32).reshape(256, NZ)
    lay_out((0, 1, 2, 13, 14, 15))
    pl.semaphore_wait(barrier, 7)
    start(0, 3, 4, 5, 6, 7, 8, 12, 13)
    lay_out(range(3, 13))
    start(2, 9, 10, 11)
    assemble(w2_ref, w2)
    start(1)

    conv_1 = functools.partial(convolve, w1, cells, 3, first, 2)
    conv_2 = functools.partial(convolve, w2, first, 2, second, 1)
    conv_up = functools.partial(refine, core, up_ref, second, fine)

    arrive(0, 2)
    conv_1(1, MIDDLE)
    arrive(12, 13)
    start(20, 21)
    arrive(3, 4)
    start(14, 15)
    arrive(5, 6)
    start(16, 17)
    arrive(7, 8)
    start(18, 19)
    start(22)
    arrive(9)
    conv_1(0, MIDDLE)
    arrive(20, 21)
    conv_1(1, BORDER)
    arrive(10)
    conv_1(-1, MIDDLE)
    start(23, 24)
    arrive(22, 1)
    conv_2(1, MIDDLE_2)
    conv_2(0, MIDDLE_2)
    start(25)
    arrive(11)
    conv_1(-2, MIDDLE)
    arrive(25)
    conv_up(1, MIDDLE_3)
    conv_2(-1, MIDDLE_2)
    conv_up(0, MIDDLE_3)
    arrive(14, 15)
    conv_1(0, BORDER)
    arrive(23, 24)
    conv_2(1, BORDER_2)
    arrive(16, 17)
    conv_1(-1, BORDER)
    start(26, 27)
    conv_2(0, BORDER_2)
    arrive(18, 19)
    conv_1(-2, BORDER)
    conv_2(-1, BORDER_2)
    arrive(26, 27)
    conv_up(1, BORDER_3)
    conv_up(0, BORDER_3)

    source = lax.broadcasted_iota(jnp.int32, (2 * NZ, 2 * NZ), 0)
    target = lax.broadcasted_iota(jnp.int32, (2 * NZ, 2 * NZ), 1)
    wanted = jnp.where(source < NZ, 2 * source, 2 * source - 2 * NZ + 1)
    interleave = jnp.where(target == wanted, 1.0, 0.0).astype(jnp.bfloat16)
    for plane in range(4):
        for part in range(4):
            lines = pl.ds(part * 128, 128)
            halves = jnp.concatenate([fine[plane, 0, lines, :], fine[plane, 1, lines, :]], axis=1)
            whole = jnp.dot(halves.astype(jnp.bfloat16), interleave, preferred_element_type=jnp.float32)
            out_ref[4 * part : 4 * part + 4, plane] = whole.astype(jnp.bfloat16).reshape(4, 32, 2 * NZ)

    for number in range(COPIES):
        copies[number].wait_send()


def per_device(field, first_weight, second_weight, up_weight):
    core = lax.rem(lax.axis_index("gx"), 2)
    taps = up_weight.transpose(2, 3, 4, 0, 1)
    taps = jnp.where(core == 0, taps, taps[::-1])
    groups = []
    for along_x in range(2):
        for along_y in range(2):
            group = taps[3 - along_x :: -2, 3 - along_y :: -2]
            groups.append(group.transpose(2, 3, 0, 1, 4).reshape(64, 4 * C))
    up = jnp.stack(groups)
    vmem = pl.BlockSpec(memory_space=pltpu.VMEM)
    return pl.pallas_call(
        kernel,
        out_shape=jax.ShapeDtypeStruct((16, 4, 32, 2 * NZ), jnp.bfloat16),
        in_specs=[vmem] * 4,
        out_specs=vmem,
        scratch_shapes=[
            pltpu.VMEM((2 * C * ROWS, NZ), jnp.float32),
            pltpu.VMEM((6, 22 * C, NZ), jnp.bfloat16),
            pltpu.VMEM((5, 20 * C, NZ), jnp.bfloat16),
            pltpu.VMEM((4, 18 * C, NZ), jnp.bfloat16),
            pltpu.VMEM((4, 2, 512, NZ), jnp.float32),
            pltpu.VMEM((192, 9 * C), jnp.bfloat16),
            pltpu.VMEM((192, 9 * C), jnp.bfloat16),
            pltpu.SemaphoreType.DMA((COPIES,)),
            pltpu.SemaphoreType.DMA((COPIES,)),
        ],
        compiler_params=pltpu.CompilerParams(
            collective_id=0, has_side_effects=True, vmem_limit_bytes=48 << 20
        ),
        name="decoder",
    )(
        field,
        first_weight.transpose(2, 3, 4, 0, 1),
        second_weight.transpose(2, 3, 4, 0, 1),
        up,
    )


def solution(mesh):
    in_specs = (
        P(None, "gx", "gy", None),
        P("col", None, None, None, None),
        P("col", None, None, None, None),
        P("col", None, None, None, None),
    )
    out_specs = P("col", "gx", "gy", None)
    return jax.shard_map(per_device, mesh=mesh, in_specs=in_specs, out_specs=out_specs, check_vma=False)
```

```python
import functools

import jax
import jax.numpy as jnp
from jax import lax
from jax.experimental import pallas as pl
from jax.experimental.pallas import tpu as pltpu
from jax.sharding import PartitionSpec as P

C = 64
NZ = 128
ROWS = 16
DEPTH = 3
MESH = pl.DeviceIdType.MESH
MIDDLE = tuple(range(1, 15))
BORDER = (-2, -1, 0, 15, 16, 17)
MIDDLE_2 = tuple(range(2, 14))
BORDER_2 = (-1, 0, 1, 14, 15, 16)
MIDDLE_3 = tuple(range(3, 13))
BORDER_3 = (0, 1, 2, 13, 14, 15)
COPIES = 28


def pairs(items):
    return [items[i : i + 2] for i in range(0, len(items), 2)]


def block(first, count):
    return pl.ds(first * C, count * C)


def taps_matmul(weight, cells, source, span):
    columns = [
        jnp.concatenate([source[layer, block(row, span), :] for layer in layers], axis=0) for layers, row in cells
    ]
    return jnp.dot(weight, jnp.concatenate(columns, axis=1), preferred_element_type=jnp.float32)


def convolve(weight_ref, source, source_at, target, target_at, layer, rows):
    weight = weight_ref[...]
    for pair in pairs(rows):
        cells = [([layer + k + source_at for k in (-1, 0, 1)], row - 1 + source_at) for row in pair]
        taps = taps_matmul(weight, cells, source, 3)
        for i, row in enumerate(pair):
            for half in range(2):
                tap = taps[half * 96 : half * 96 + 96, i * NZ : (i + 1) * NZ]
                value = pltpu.roll(tap[:32], 1, 1) + tap[32:64] + pltpu.roll(tap[64:], NZ - 1, 1)
                start = (row + target_at) * C + half * 32
                target[layer + target_at, start : start + 32, :] = jnp.maximum(value, 0.0).astype(jnp.bfloat16)


def refine(core, weight_ref, source, fine, layer, rows):
    for along_x in range(2):
        flat = 2 * layer + along_x
        plane = flat + core * (3 - 2 * flat)
        for along_y in range(2):
            weight = weight_ref[2 * along_x + along_y]
            for pair in pairs(rows):
                cells = [([layer + along_x, layer + along_x + 1], row + along_y) for row in pair]
                taps = taps_matmul(weight, cells, source, 2)
                for i, row in enumerate(pair):
                    tap = taps[:, i * NZ : (i + 1) * NZ]
                    even = pltpu.roll(tap[48:], 1, 1) + tap[16:32]
                    odd = tap[32:48] + pltpu.roll(tap[:16], NZ - 1, 1)
                    line = pl.ds(2 * row + along_y, 16, stride=32)
                    fine[plane, 0, line, :] = even
                    fine[plane, 1, line, :] = odd


def kernel(
    field_in, w1_in, w2_in, up_in, out,
    field_ref, w1_ref, w2_ref, up_ref, out_ref,
    spread, cells, first, second, fine, w1, w2, up_taps, up_weight, send, recv, load, store,
):
    gx = lax.axis_index("gx")
    gy = lax.axis_index("gy")
    col = lax.axis_index("col")
    core = lax.rem(gx, 2)
    sign = 1 - 2 * core
    partner = {"gx": gx + sign}
    outer = {"gx": lax.rem(gx + 16 - sign, 16)}
    far = {"gx": lax.rem(gx + 16 + 2 * sign, 16)}
    far_back = {"gx": lax.rem(gx + 16 - 2 * sign, 16)}
    up = {"gy": lax.rem(gy + 1, 8)}
    down = {"gy": lax.rem(gy + 7, 8)}
    other = {"col": 1 - col}

    barrier = pltpu.get_barrier_semaphore()
    for device in (partner, outer, far, far_back, up, down, other):
        pl.semaphore_signal(barrier, inc=1, device_id=device, device_id_type=MESH)

    loads = [
        pltpu.make_async_copy(source, target, load.at[i])
        for i, (source, target) in enumerate(
            ((field_in, field_ref), (w1_in, w1_ref), (w2_in, w2_ref), (up_in, up_ref))
        )
    ]
    for local in loads:
        local.start()

    def copy(number, source, target, device):
        return pltpu.make_async_remote_copy(
            src_ref=source,
            dst_ref=target,
            send_sem=send.at[number],
            recv_sem=recv.at[number],
            device_id=device,
            device_id_type=MESH,
        )

    def rows_of(buffer, at, source_layer, source_row, target_layer, target_row, count):
        return (
            buffer.at[source_layer + at, block(source_row + at, count)],
            buffer.at[target_layer + at, block(target_row + at, count)],
        )

    mine = pl.ds(pl.multiple_of(col * 96, 96), 96)

    def same(ref):
        return ref.at[mine], ref.at[mine]

    a = functools.partial(rows_of, cells, 3)
    f = functools.partial(rows_of, first, 2)
    s = functools.partial(rows_of, second, 1)
    both = pl.ds(3, 2)
    copies = [
        copy(0, *same(w1), other),
        copy(1, *same(w2), other),
        copy(2, *a(1, 0, 2, 0, 16), partner),
        copy(3, *a(0, 0, -1, 0, 3), outer),
        copy(4, *a(0, 13, -1, 13, 3), outer),
        copy(5, *a(1, 0, -2, 0, 3), outer),
        copy(6, *a(1, 13, -2, 13, 3), outer),
        copy(7, *a(1, 0, -3, 0, 3), far),
        copy(8, *a(1, 13, -3, 13, 3), far),
        copy(9, *a(0, 3, -1, 3, 10), outer),
        copy(10, *a(1, 3, -2, 3, 10), outer),
        copy(11, *a(1, 3, -3, 3, 10), far),
        copy(12, cells.at[both, block(3, 3)], cells.at[both, block(19, 3)], down),
        copy(13, cells.at[both, block(16, 3)], cells.at[both, block(0, 3)], up),
        copy(14, *a(-1, 0, -1, 16, 3), down),
        copy(15, *a(-1, 13, -1, -3, 3), up),
        copy(16, *a(-2, 0, -2, 16, 3), down),
        copy(17, *a(-2, 13, -2, -3, 3), up),
        copy(18, *a(-3, 0, -3, 16, 3), down),
        copy(19, *a(-3, 13, -3, -3, 3), up),
        copy(20, *a(1, -3, 2, -3, 3), partner),
        copy(21, *a(1, 16, 2, 16, 3), partner),
        copy(22, *f(1, 1, 2, 1, 14), partner),
        copy(23, *f(1, -2, 2, -2, 3), partner),
        copy(24, *f(1, 15, 2, 15, 3), partner),
        copy(25, *s(1, 2, 2, 2, 12), partner),
        copy(26, *s(1, -1, 2, -1, 3), partner),
        copy(27, *s(1, 14, 2, 14, 3), partner),
    ]

    def start(*numbers):
        for number in numbers:
            copies[number].start()

    def arrive(*numbers):
        for number in numbers:
            copies[number].wait_recv()

    def assemble(source, target):
        for along_x in range(3):
            for along_y in range(3):
                piece = source[along_x + core * (2 - 2 * along_x), along_y].reshape(96, C)
                k = 3 * along_x + along_y
                target[mine, k * C : (k + 1) * C] = piece

    def assemble_up():
        for along_x in range(4):
            for o in range(16):
                piece = up_ref[o, along_x + core * (3 - 2 * along_x)].astype(jnp.float32)
                for along_y in range(4):
                    up_taps[4 * along_x + along_y, 4 * o : 4 * o + 4, :] = piece[along_y]
        for x in range(4):
            for y in range(4):
                k = 2 * (1 - x // 2) + 1 - y // 2
                for z in range(4):
                    value = up_taps[4 * x + y, pl.ds(z, 16, stride=4), :]
                    up_weight[2 * ((3 - x) % 2) + (3 - y) % 2, 16 * z : 16 * z + 16, k * C : (k + 1) * C] = (
                        value.astype(jnp.bfloat16)
                    )

    def lay_out(rows):
        for layer in range(2):
            plane = layer + core * (1 - 2 * layer)
            for row in rows:
                value = spread[pl.ds(plane * ROWS + row, C, stride=2 * ROWS), :]
                cells[layer + 3, block(row + 3, 1), :] = value.astype(jnp.bfloat16)

    loads[1].wait()
    assemble(w1_ref, w1)
    loads[0].wait()
    for i in range(8):
        spread[i * 256 : (i + 1) * 256, :] = field_ref[8 * i : 8 * i + 8].astype(jnp.float32).reshape(256, NZ)
    lay_out((0, 1, 2, 13, 14, 15))
    pl.semaphore_wait(barrier, 7)
    start(0, 3, 4, 5, 6, 7, 8, 12, 13)
    lay_out(range(3, 13))
    start(2, 9, 10, 11)
    loads[2].wait()
    assemble(w2_ref, w2)
    start(1)
    loads[3].wait()
    assemble_up()

    conv_1 = functools.partial(convolve, w1, cells, 3, first, 2)
    conv_2 = functools.partial(convolve, w2, first, 2, second, 1)
    conv_up = functools.partial(refine, core, up_weight, second, fine)

    arrive(0, 2)
    conv_1(1, MIDDLE)
    arrive(12, 13)
    start(20, 21)
    arrive(3, 4)
    start(14, 15)
    arrive(5, 6)
    start(16, 17)
    arrive(7, 8)
    start(18, 19)
    start(22)
    arrive(9)
    conv_1(0, MIDDLE)
    arrive(20, 21)
    conv_1(1, BORDER)
    arrive(10)
    conv_1(-1, MIDDLE)
    start(23, 24)
    arrive(22, 1)
    conv_2(1, MIDDLE_2)
    conv_2(0, MIDDLE_2)
    start(25)
    arrive(11)
    conv_1(-2, MIDDLE)
    arrive(25)
    conv_up(1, MIDDLE_3)
    conv_2(-1, MIDDLE_2)
    conv_up(0, MIDDLE_3)
    arrive(14, 15)
    conv_1(0, BORDER)
    arrive(23, 24)
    conv_2(1, BORDER_2)
    arrive(16, 17)
    conv_1(-1, BORDER)
    start(26, 27)
    conv_2(0, BORDER_2)
    arrive(18, 19)
    conv_1(-2, BORDER)
    conv_2(-1, BORDER_2)
    arrive(26, 27)
    conv_up(1, BORDER_3)
    conv_up(0, BORDER_3)

    source = lax.broadcasted_iota(jnp.int32, (2 * NZ, 2 * NZ), 0)
    target = lax.broadcasted_iota(jnp.int32, (2 * NZ, 2 * NZ), 1)
    wanted = jnp.where(source < NZ, 2 * source, 2 * source - 2 * NZ + 1)
    interleave = jnp.where(target == wanted, 1.0, 0.0).astype(jnp.bfloat16)
    stores = []
    for plane in range(4):
        for part in range(4):
            lines = pl.ds(part * 128, 128)
            halves = jnp.concatenate([fine[plane, 0, lines, :], fine[plane, 1, lines, :]], axis=1)
            whole = jnp.dot(halves.astype(jnp.bfloat16), interleave, preferred_element_type=jnp.float32)
            out_ref[4 * part : 4 * part + 4, plane] = whole.astype(jnp.bfloat16).reshape(4, 32, 2 * NZ)
        stores.append(pltpu.make_async_copy(out_ref.at[:, plane], out.at[:, plane], store.at[plane]))
        stores[plane].start()

    for number in range(COPIES):
        copies[number].wait_send()
    for local in stores:
        local.wait()


def per_device(field, first_weight, second_weight, up_weight):
    hbm = pl.BlockSpec(memory_space=pltpu.HBM)
    return pl.pallas_call(
        kernel,
        out_shape=pltpu.HBM((16, 4, 32, 2 * NZ), jnp.bfloat16),
        in_specs=[hbm] * 4,
        out_specs=hbm,
        scratch_shapes=[
            pltpu.VMEM((C, 2, ROWS, NZ), jnp.bfloat16),
            pltpu.VMEM((3, 3, 3, 32, C), jnp.bfloat16),
            pltpu.VMEM((3, 3, 3, 32, C), jnp.bfloat16),
            pltpu.VMEM((16, 4, 4, 4, C), jnp.bfloat16),
            pltpu.VMEM((16, 4, 32, 2 * NZ), jnp.bfloat16),
            pltpu.VMEM((2 * C * ROWS, NZ), jnp.float32),
            pltpu.VMEM((6, 22 * C, NZ), jnp.bfloat16),
            pltpu.VMEM((5, 20 * C, NZ), jnp.bfloat16),
            pltpu.VMEM((4, 18 * C, NZ), jnp.bfloat16),
            pltpu.VMEM((4, 2, 512, NZ), jnp.float32),
            pltpu.VMEM((192, 9 * C), jnp.bfloat16),
            pltpu.VMEM((192, 9 * C), jnp.bfloat16),
            pltpu.VMEM((16, C, C), jnp.float32),
            pltpu.VMEM((4, C, 4 * C), jnp.bfloat16),
            pltpu.SemaphoreType.DMA((COPIES,)),
            pltpu.SemaphoreType.DMA((COPIES,)),
            pltpu.SemaphoreType.DMA((4,)),
            pltpu.SemaphoreType.DMA((4,)),
        ],
        compiler_params=pltpu.CompilerParams(
            collective_id=0, has_side_effects=True, vmem_limit_bytes=48 << 20
        ),
        name="decoder",
    )(
        *(
            pltpu.with_memory_space_constraint(value, pltpu.HBM)
            for value in (
                field,
                first_weight.transpose(2, 3, 4, 0, 1),
                second_weight.transpose(2, 3, 4, 0, 1),
                up_weight.transpose(0, 2, 3, 4, 1),
            )
        )
    )


def solution(mesh):
    in_specs = (
        P(None, "gx", "gy", None),
        P("col", None, None, None, None),
        P("col", None, None, None, None),
        P("col", None, None, None, None),
    )
    out_specs = P("col", "gx", "gy", None)
    return jax.shard_map(per_device, mesh=mesh, in_specs=in_specs, out_specs=out_specs, check_vma=False)
```

```python
import functools

import jax
import jax.numpy as jnp
from jax import lax
from jax.experimental import pallas as pl
from jax.experimental.pallas import tpu as pltpu
from jax.sharding import PartitionSpec as P

C = 64
NZ = 128
ROWS = 16
DEPTH = 3
MESH = pl.DeviceIdType.MESH
MIDDLE = tuple(range(1, 15))
BORDER = (-2, -1, 0, 15, 16, 17)
MIDDLE_2 = tuple(range(2, 14))
BORDER_2 = (-1, 0, 1, 14, 15, 16)
MIDDLE_3 = tuple(range(3, 13))
BORDER_3 = (0, 1, 2, 13, 14, 15)
COPIES = 28


def pairs(items):
    return [items[i : i + 2] for i in range(0, len(items), 2)]


def block(first, count):
    return pl.ds(first * C, count * C)


def taps_matmul(weight, cells, source, span):
    columns = [
        jnp.concatenate([source[layer, block(row, span), :] for layer in layers], axis=0) for layers, row in cells
    ]
    return jnp.dot(weight, jnp.concatenate(columns, axis=1), preferred_element_type=jnp.float32)


def convolve(weight_ref, source, source_at, target, target_at, layer, rows):
    weight = weight_ref[...]
    for pair in pairs(rows):
        cells = [([layer + k + source_at for k in (-1, 0, 1)], row - 1 + source_at) for row in pair]
        taps = taps_matmul(weight, cells, source, 3)
        for i, row in enumerate(pair):
            for half in range(2):
                tap = taps[half * 96 : half * 96 + 96, i * NZ : (i + 1) * NZ]
                value = pltpu.roll(tap[:32], 1, 1) + tap[32:64] + pltpu.roll(tap[64:], NZ - 1, 1)
                start = (row + target_at) * C + half * 32
                target[layer + target_at, start : start + 32, :] = jnp.maximum(value, 0.0).astype(jnp.bfloat16)


def refine(core, weight_ref, source, fine, layer, rows):
    for along_x in range(2):
        flat = 2 * layer + along_x
        plane = flat + core * (3 - 2 * flat)
        for along_y in range(2):
            weight = weight_ref[2 * along_x + along_y]
            for pair in pairs(rows):
                cells = [([layer + along_x, layer + along_x + 1], row + along_y) for row in pair]
                taps = taps_matmul(weight, cells, source, 2)
                for i, row in enumerate(pair):
                    tap = taps[:, i * NZ : (i + 1) * NZ]
                    even = pltpu.roll(tap[48:], 1, 1) + tap[16:32]
                    odd = tap[32:48] + pltpu.roll(tap[:16], NZ - 1, 1)
                    line = pl.ds(2 * row + along_y, 16, stride=32)
                    fine[plane, 0, line, :] = even
                    fine[plane, 1, line, :] = odd


def kernel(
    field_in, w1_in, w2_in, up_in, out_ref,
    field_ref, w1_ref, w2_ref, up_ref,
    spread, cells, first, second, fine, w1, w2, up_taps, up_weight, send, recv, load,
):
    gx = lax.axis_index("gx")
    gy = lax.axis_index("gy")
    col = lax.axis_index("col")
    core = lax.rem(gx, 2)
    sign = 1 - 2 * core
    partner = {"gx": gx + sign}
    outer = {"gx": lax.rem(gx + 16 - sign, 16)}
    far = {"gx": lax.rem(gx + 16 + 2 * sign, 16)}
    far_back = {"gx": lax.rem(gx + 16 - 2 * sign, 16)}
    up = {"gy": lax.rem(gy + 1, 8)}
    down = {"gy": lax.rem(gy + 7, 8)}
    other = {"col": 1 - col}

    barrier = pltpu.get_barrier_semaphore()
    for device in (partner, outer, far, far_back, up, down, other):
        pl.semaphore_signal(barrier, inc=1, device_id=device, device_id_type=MESH)

    loads = [
        pltpu.make_async_copy(source, target, load.at[i])
        for i, (source, target) in enumerate(
            ((field_in, field_ref), (w1_in, w1_ref), (w2_in, w2_ref), (up_in, up_ref))
        )
    ]
    for local in loads:
        local.start()

    def copy(number, source, target, device):
        return pltpu.make_async_remote_copy(
            src_ref=source,
            dst_ref=target,
            send_sem=send.at[number],
            recv_sem=recv.at[number],
            device_id=device,
            device_id_type=MESH,
        )

    def rows_of(buffer, at, source_layer, source_row, target_layer, target_row, count):
        return (
            buffer.at[source_layer + at, block(source_row + at, count)],
            buffer.at[target_layer + at, block(target_row + at, count)],
        )

    mine = pl.ds(pl.multiple_of(col * 96, 96), 96)

    def same(ref):
        return ref.at[mine], ref.at[mine]

    a = functools.partial(rows_of, cells, 3)
    f = functools.partial(rows_of, first, 2)
    s = functools.partial(rows_of, second, 1)
    both = pl.ds(3, 2)
    copies = [
        copy(0, *same(w1), other),
        copy(1, *same(w2), other),
        copy(2, *a(1, 0, 2, 0, 16), partner),
        copy(3, *a(0, 0, -1, 0, 3), outer),
        copy(4, *a(0, 13, -1, 13, 3), outer),
        copy(5, *a(1, 0, -2, 0, 3), outer),
        copy(6, *a(1, 13, -2, 13, 3), outer),
        copy(7, *a(1, 0, -3, 0, 3), far),
        copy(8, *a(1, 13, -3, 13, 3), far),
        copy(9, *a(0, 3, -1, 3, 10), outer),
        copy(10, *a(1, 3, -2, 3, 10), outer),
        copy(11, *a(1, 3, -3, 3, 10), far),
        copy(12, cells.at[both, block(3, 3)], cells.at[both, block(19, 3)], down),
        copy(13, cells.at[both, block(16, 3)], cells.at[both, block(0, 3)], up),
        copy(14, *a(-1, 0, -1, 16, 3), down),
        copy(15, *a(-1, 13, -1, -3, 3), up),
        copy(16, *a(-2, 0, -2, 16, 3), down),
        copy(17, *a(-2, 13, -2, -3, 3), up),
        copy(18, *a(-3, 0, -3, 16, 3), down),
        copy(19, *a(-3, 13, -3, -3, 3), up),
        copy(20, *a(1, -3, 2, -3, 3), partner),
        copy(21, *a(1, 16, 2, 16, 3), partner),
        copy(22, *f(1, 1, 2, 1, 14), partner),
        copy(23, *f(1, -2, 2, -2, 3), partner),
        copy(24, *f(1, 15, 2, 15, 3), partner),
        copy(25, *s(1, 2, 2, 2, 12), partner),
        copy(26, *s(1, -1, 2, -1, 3), partner),
        copy(27, *s(1, 14, 2, 14, 3), partner),
    ]

    def start(*numbers):
        for number in numbers:
            copies[number].start()

    def arrive(*numbers):
        for number in numbers:
            copies[number].wait_recv()

    def assemble(source, target):
        for along_x in range(3):
            for along_y in range(3):
                piece = source[along_x + core * (2 - 2 * along_x), along_y].reshape(96, C)
                k = 3 * along_x + along_y
                target[mine, k * C : (k + 1) * C] = piece

    def assemble_up():
        for along_x in range(4):
            for o in range(16):
                piece = up_ref[o, along_x + core * (3 - 2 * along_x)].astype(jnp.float32)
                for along_y in range(4):
                    up_taps[4 * along_x + along_y, 4 * o : 4 * o + 4, :] = piece[along_y]
        for x in range(4):
            for y in range(4):
                k = 2 * (1 - x // 2) + 1 - y // 2
                for z in range(4):
                    value = up_taps[4 * x + y, pl.ds(z, 16, stride=4), :]
                    up_weight[2 * ((3 - x) % 2) + (3 - y) % 2, 16 * z : 16 * z + 16, k * C : (k + 1) * C] = (
                        value.astype(jnp.bfloat16)
                    )

    def lay_out(rows):
        for layer in range(2):
            plane = layer + core * (1 - 2 * layer)
            for row in rows:
                value = spread[pl.ds(plane * ROWS + row, C, stride=2 * ROWS), :]
                cells[layer + 3, block(row + 3, 1), :] = value.astype(jnp.bfloat16)

    loads[1].wait()
    assemble(w1_ref, w1)
    loads[0].wait()
    for i in range(8):
        spread[i * 256 : (i + 1) * 256, :] = field_ref[8 * i : 8 * i + 8].astype(jnp.float32).reshape(256, NZ)
    lay_out((0, 1, 2, 13, 14, 15))
    pl.semaphore_wait(barrier, 7)
    start(0, 3, 4, 5, 6, 7, 8, 12, 13)
    lay_out(range(3, 13))
    start(2, 9, 10, 11)
    loads[2].wait()
    assemble(w2_ref, w2)
    start(1)
    loads[3].wait()

    conv_1 = functools.partial(convolve, w1, cells, 3, first, 2)
    conv_2 = functools.partial(convolve, w2, first, 2, second, 1)
    conv_up = functools.partial(refine, core, up_weight, second, fine)

    source = lax.broadcasted_iota(jnp.int32, (2 * NZ, 2 * NZ), 0)
    target = lax.broadcasted_iota(jnp.int32, (2 * NZ, 2 * NZ), 1)
    wanted = jnp.where(source < NZ, 2 * source, 2 * source - 2 * NZ + 1)
    interleave = jnp.where(target == wanted, 1.0, 0.0).astype(jnp.bfloat16)

    def weave(layer):
        for flat in (2 * layer, 2 * layer + 1):
            plane = flat + core * (3 - 2 * flat)
            for part in range(4):
                lines = pl.ds(part * 128, 128)
                halves = jnp.concatenate([fine[plane, 0, lines, :], fine[plane, 1, lines, :]], axis=1)
                whole = jnp.dot(halves.astype(jnp.bfloat16), interleave, preferred_element_type=jnp.float32)
                out_ref[4 * part : 4 * part + 4, plane] = whole.astype(jnp.bfloat16).reshape(4, 32, 2 * NZ)

    arrive(0, 2)
    conv_1(1, MIDDLE)
    start(22)
    arrive(12, 13)
    start(20, 21)
    arrive(3, 4)
    start(14, 15)
    arrive(5, 6)
    start(16, 17)
    arrive(7, 8)
    start(18, 19)
    assemble_up()
    arrive(20, 21)
    conv_1(1, BORDER)
    start(23, 24)
    arrive(9)
    conv_1(0, MIDDLE)
    arrive(22, 1)
    conv_2(1, MIDDLE_2)
    start(25)
    arrive(14, 15)
    conv_1(0, BORDER)
    arrive(23, 24)
    conv_2(1, BORDER_2)
    start(26, 27)
    arrive(10)
    conv_1(-1, MIDDLE)
    conv_2(0, MIDDLE_2)
    arrive(25)
    conv_up(1, MIDDLE_3)
    arrive(16, 17)
    conv_1(-1, BORDER)
    conv_2(0, BORDER_2)
    arrive(26, 27)
    conv_up(1, BORDER_3)
    weave(1)
    arrive(11)
    conv_1(-2, MIDDLE)
    arrive(18, 19)
    conv_1(-2, BORDER)
    conv_2(-1, MIDDLE_2)
    conv_2(-1, BORDER_2)
    conv_up(0, MIDDLE_3)
    conv_up(0, BORDER_3)
    weave(0)

    for number in range(COPIES):
        copies[number].wait_send()


def per_device(field, first_weight, second_weight, up_weight):
    hbm = pl.BlockSpec(memory_space=pltpu.HBM)
    return pl.pallas_call(
        kernel,
        out_shape=jax.ShapeDtypeStruct((16, 4, 32, 2 * NZ), jnp.bfloat16),
        in_specs=[hbm] * 4,
        out_specs=pl.BlockSpec(memory_space=pltpu.VMEM),
        scratch_shapes=[
            pltpu.VMEM((C, 2, ROWS, NZ), jnp.bfloat16),
            pltpu.VMEM((3, 3, 3, 32, C), jnp.bfloat16),
            pltpu.VMEM((3, 3, 3, 32, C), jnp.bfloat16),
            pltpu.VMEM((16, 4, 4, 4, C), jnp.bfloat16),
            pltpu.VMEM((2 * C * ROWS, NZ), jnp.float32),
            pltpu.VMEM((6, 22 * C, NZ), jnp.bfloat16),
            pltpu.VMEM((5, 20 * C, NZ), jnp.bfloat16),
            pltpu.VMEM((4, 18 * C, NZ), jnp.bfloat16),
            pltpu.VMEM((4, 2, 512, NZ), jnp.float32),
            pltpu.VMEM((192, 9 * C), jnp.bfloat16),
            pltpu.VMEM((192, 9 * C), jnp.bfloat16),
            pltpu.VMEM((16, C, C), jnp.float32),
            pltpu.VMEM((4, C, 4 * C), jnp.bfloat16),
            pltpu.SemaphoreType.DMA((COPIES,)),
            pltpu.SemaphoreType.DMA((COPIES,)),
            pltpu.SemaphoreType.DMA((4,)),
        ],
        compiler_params=pltpu.CompilerParams(
            collective_id=0, has_side_effects=True, vmem_limit_bytes=48 << 20
        ),
        name="decoder",
    )(
        *(
            pltpu.with_memory_space_constraint(value, pltpu.HBM)
            for value in (
                field,
                first_weight.transpose(2, 3, 4, 0, 1),
                second_weight.transpose(2, 3, 4, 0, 1),
                up_weight.transpose(0, 2, 3, 4, 1),
            )
        )
    )


def solution(mesh):
    in_specs = (
        P(None, "gx", "gy", None),
        P("col", None, None, None, None),
        P("col", None, None, None, None),
        P("col", None, None, None, None),
    )
    out_specs = P("col", "gx", "gy", None)
    return jax.shard_map(per_device, mesh=mesh, in_specs=in_specs, out_specs=out_specs, check_vma=False)
```
